128 devices in a mesh: dp: 4 (over y), expert: 32 (over z, x, core).
Axes of the slice: x: 4, y: 4, z: 4, core: 2. Of those that a mesh axis runs over, the one named last changes fastest.
Arguments:
- tokens: bfloat16 [16384, 2048], P(('dp', 'expert')), may hold values from -6 to 6
- expert_ids: int32 [16384, 8], P(('dp', 'expert')), may hold values from 0 to 63, all different within a row
- bucket_codes: int32 [16384, 8], P(('dp', 'expert')), may hold values from 0 to 65535
- route_weights: float32 [16384, 8], P(('dp', 'expert')), may hold values from 0.1 to 1
- cotangent: bfloat16 [16384, 2048], P(('dp', 'expert')), may hold values from -2 to 2
- counts: int32 [64], replicated, may hold values from 4 to 16, as said below
- comp_scale: bfloat16 [64, 2048], replicated, may hold values from -3 to 3
- w_gate: bfloat16 [64, 2048, 768], P('expert'), may hold values from -0.125 to 0.125
- w_up: bfloat16 [64, 2048, 768], P('expert'), may hold values from -0.125 to 0.125
- w_down: bfloat16 [64, 768, 2048], P('expert'), may hold values from -0.21875 to 0.21875
Outputs:
- layer_output: bfloat16 [16384, 2048], P(('dp', 'expert'))
- grad_tokens: bfloat16 [16384, 2048], P(('dp', 'expert'))
- grad_down: bfloat16 [64, 768, 2048], P('expert', None, 'dp')
The draws below stay inside these ranges and needn't reach their ends.
Inputs may be any that keep to these rules, and one draw needn't show every extreme that they name: `counts`: experts 2i and 2i+1 (those of index i of the expert axis) have 20 buckets together; some expert has exactly 16. `expert_ids`: the 8 experts of one token differ.
All inputs are finite; a program needn't handle non-finite values.
Results may differ from the reference program's by a relative error of at most 0.013.
Values may be sent and summed in bfloat16 or wider, within the bound.
A program may use at most 192 MiB of HBM per device.

```python
import jax
import jax.numpy as jnp
from jax import lax

D = 2048
FF = 768
TOPK = 8
NB = 16
BUCKET_DEV = 20
TOK_DEV = 128
EXPERTS = 64
TOKENS = 16384
N_DP = 4
N_EXPERT = 32


def draw_counts(key, part):
    half_total = EXPERTS // 2
    first_key = jax.random.fold_in(key, 11)
    pick_key = jax.random.fold_in(key, 12)
    first_count = jax.random.randint(first_key, (half_total,), BUCKET_DEV - NB, NB + 1, dtype=jnp.int32)
    chosen = jax.random.randint(pick_key, (), 0, half_total, dtype=jnp.int32)
    first_count = jnp.where(jnp.arange(half_total, dtype=jnp.int32) == chosen, NB, first_count)
    second_count = BUCKET_DEV - first_count
    return jnp.stack([first_count, second_count], axis=1).reshape(EXPERTS).astype(jnp.int32)


def with_ends(values, rng, least, high):
    longest = values.shape.index(max(values.shape))
    spots = []
    for shift in (0, 1):
        where = [jax.random.randint(jax.random.fold_in(rng, axis), (), 0, length) for axis, length in enumerate(values.shape)]
        where[longest] = (where[longest] + shift) % values.shape[longest]
        spots.append(tuple(where))
    return values.at[spots[0]].set(least).at[spots[1]].set(high)


def block_scale(rng, shape, pieces, least, high):
    level = 1.0
    for dim, parts in pieces:
        draws = jax.random.uniform(jax.random.fold_in(jax.random.fold_in(rng, 6), dim), (parts,), jnp.float32, least / len(pieces), high / len(pieces))
        level = level * jnp.repeat(jnp.exp(draws), shape[dim] // parts).reshape((-1,) + (1,) * (len(shape) - 1 - dim))
    return level


def choose_distinct(own_key, rows, count, top, lift):
    ranking = jax.random.permutation(jax.random.fold_in(own_key, 1), count)
    favour = ranking
    for power in range(3):
        favour = favour * favour // count
    favour = favour * lift // count
    chance = jax.random.randint(jax.random.fold_in(own_key, 2), (rows, count), 0, 4096) + favour
    fixed_rows = jax.random.permutation(jax.random.fold_in(own_key, 3), rows)[jnp.arange(count) % rows]
    chance = jnp.where(jnp.arange(rows)[:, None] == fixed_rows[None, :], 1 << 14, chance)
    score = chance * count + jnp.arange(count)
    return lax.top_k(score.astype(jnp.int32), top)[1].astype(jnp.int32)


def normal_values(rng, shape, scale, most, cuts=(), kind=jnp.bfloat16):
    array = scale * jax.random.normal(rng, shape, jnp.float32)
    if cuts:
        array = array * block_scale(rng, shape, cuts, -0.22, 0.18)
    return jnp.clip(array, -most, most).astype(kind)


def setup_inputs(seed: int = 0) -> dict:
    arg_keys = jax.random.split(jax.random.key(seed), 11)
    tokens = normal_values(arg_keys[0], (TOKENS, D), 1.0, 6.0, ((0, 128),))
    expert_ids = choose_distinct(arg_keys[1], TOKENS, EXPERTS, TOPK, 2048)
    bucket_codes = with_ends(jax.random.randint(arg_keys[2], (TOKENS, TOPK), 0, 65536), jax.random.fold_in(arg_keys[2], 1), 0, 65535).astype(jnp.int32)
    route_weights = jnp.clip(0.1 + 0.9 * jax.random.uniform(arg_keys[3], (TOKENS, TOPK), jnp.float32) ** block_scale(arg_keys[3], (TOKENS, TOPK), ((0, 128),), -0.2, 0.2), 0.1, 1.0)
    cotangent = normal_values(arg_keys[4], (TOKENS, D), 0.3, 2.0, ((0, 128),))
    counts = draw_counts(jax.random.fold_in(arg_keys[10], 71), 0)
    comp_scale = normal_values(arg_keys[6], (EXPERTS, D), 0.5, 3.0)
    w_gate = normal_values(arg_keys[7], (EXPERTS, D, FF), D ** -0.5, 0.125, ((0, 32),))
    w_up = normal_values(arg_keys[8], (EXPERTS, D, FF), D ** -0.5, 0.125, ((0, 32),))
    w_down = normal_values(arg_keys[9], (EXPERTS, FF, D), FF ** -0.5, 0.21875, ((0, 32),))
    return {"tokens": tokens, "expert_ids": expert_ids, "bucket_codes": bucket_codes, "route_weights": route_weights, "cotangent": cotangent, "counts": counts, "comp_scale": comp_scale, "w_gate": w_gate, "w_up": w_up, "w_down": w_down}


def reference(tokens, expert_ids, bucket_codes, route_weights, cotangent, counts, comp_scale, w_gate, w_up, w_down):
    sources = N_DP * N_EXPERT
    slot_total = EXPERTS * NB
    tok_blocks = tokens.reshape(sources, TOK_DEV, D)
    id_blocks = expert_ids.reshape(sources, TOK_DEV, TOPK)
    code_blocks = bucket_codes.reshape(sources, TOK_DEV, TOPK)
    weight_blocks = route_weights.reshape(sources, TOK_DEV, TOPK)
    cot_blocks = cotangent.reshape(sources, TOK_DEV, D)

    def slot_of(id_block, code_block):
        pair_count = counts[id_block]
        return (id_block * NB + code_block % pair_count).astype(jnp.int32)

    def build(block):
        tok_block, id_block, code_block, weight_block, cot_block = block
        slot_id = slot_of(id_block, code_block)
        slot_hit = (slot_id[:, :, None] == jnp.arange(slot_total, dtype=jnp.int32)).astype(jnp.float32)
        member = jnp.sum(slot_hit, axis=1).T
        weighted = jnp.sum(slot_hit * weight_block[:, :, None], axis=1).T
        occupancy = jnp.sum(member, axis=1)
        bucket_sums = jnp.dot(member, tok_block.astype(jnp.float32), precision=lax.Precision.HIGHEST)
        centroid = (bucket_sums / jnp.maximum(occupancy, 1.0)[:, None]).astype(jnp.bfloat16)
        pull_sum = jnp.dot(weighted, cot_block.astype(jnp.float32), precision=lax.Precision.HIGHEST).astype(jnp.bfloat16)
        return centroid, pull_sum, occupancy

    centroids, pulls, occupancies = lax.map(build, (tok_blocks, id_blocks, code_blocks, weight_blocks, cot_blocks))
    cent_four = centroids.reshape(sources, EXPERTS, NB, D)
    pull_four = pulls.reshape(sources, EXPERTS, NB, D)

    def expert_step(index):
        arrived = lax.dynamic_index_in_dim(cent_four, index, axis=1, keepdims=False).reshape(sources * NB, D)
        pull_rows = lax.dynamic_index_in_dim(pull_four, index, axis=1, keepdims=False).reshape(sources * NB, D)
        gate_weight = lax.dynamic_index_in_dim(w_gate, index, axis=0, keepdims=False)
        up_weight = lax.dynamic_index_in_dim(w_up, index, axis=0, keepdims=False)
        down_weight = lax.dynamic_index_in_dim(w_down, index, axis=0, keepdims=False)
        gate_act = jnp.dot(arrived, gate_weight, preferred_element_type=jnp.float32)
        up_act = jnp.dot(arrived, up_weight, preferred_element_type=jnp.float32)
        gate_sigmoid = jax.nn.sigmoid(gate_act)
        hidden = (gate_act * gate_sigmoid * up_act).astype(jnp.bfloat16)
        expert_out = jnp.dot(hidden, down_weight, preferred_element_type=jnp.float32).astype(jnp.bfloat16)
        d_hidden = jnp.dot(pull_rows, down_weight.T, preferred_element_type=jnp.float32)
        d_gate = (d_hidden * up_act * gate_sigmoid * (1.0 + gate_act * (1.0 - gate_sigmoid))).astype(jnp.bfloat16)
        d_up = (d_hidden * gate_act * gate_sigmoid).astype(jnp.bfloat16)
        back_rows = (jnp.dot(d_gate, gate_weight.T, preferred_element_type=jnp.float32)
                     + jnp.dot(d_up, up_weight.T, preferred_element_type=jnp.float32)).astype(jnp.bfloat16)
        hidden_groups = hidden.reshape(N_DP, N_EXPERT * NB, FF).astype(jnp.float32)
        pull_groups = pull_rows.reshape(N_DP, N_EXPERT * NB, D).astype(jnp.float32)
        partial_grad = jnp.einsum("pqf,pqd->pfd", hidden_groups, pull_groups, precision=lax.Precision.HIGHEST)
        rounded = lax.optimization_barrier(partial_grad.astype(jnp.bfloat16)).astype(jnp.float32)
        grad_expert = jnp.sum(rounded, axis=0).astype(jnp.bfloat16)
        return expert_out.reshape(sources, NB, D), back_rows.reshape(sources, NB, D), grad_expert

    outs, backs, grad_down = lax.map(expert_step, jnp.arange(EXPERTS, dtype=jnp.int32))
    out_blocks = jnp.transpose(outs, (1, 0, 2, 3)).reshape(sources, slot_total, D)
    back_blocks = jnp.transpose(backs, (1, 0, 2, 3)).reshape(sources, slot_total, D)

    def combine(block):
        tok_block, id_block, code_block, weight_block, cot_block, cent_block, pull_block, out_block, back_block, occ_block = block
        slot_id = slot_of(id_block, code_block)
        out_pair = out_block[slot_id].astype(jnp.float32)
        cent_pair = cent_block[slot_id].astype(jnp.float32)
        pull_pair = pull_block[slot_id].astype(jnp.float32)
        back_pair = back_block[slot_id].astype(jnp.float32)
        occ_pair = jnp.maximum(occ_block[slot_id], 1.0)
        scale_pair = comp_scale[id_block].astype(jnp.float32)
        route_pair = weight_block[:, :, None]
        layer = jnp.sum(route_pair * (out_pair + scale_pair * (tok_block.astype(jnp.float32)[:, None, :] - cent_pair)), axis=1)
        grad_tok = jnp.sum(route_pair * scale_pair * cot_block.astype(jnp.float32)[:, None, :]
                           + (back_pair - scale_pair * pull_pair) / occ_pair[:, :, None], axis=1)
        return layer.astype(jnp.bfloat16), grad_tok.astype(jnp.bfloat16)

    layers, grads = lax.map(combine, (tok_blocks, id_blocks, code_blocks, weight_blocks, cot_blocks,
                                      centroids, pulls, out_blocks, back_blocks, occupancies))
    return layers.reshape(TOKENS, D), grads.reshape(TOKENS, D), grad_down
```

```python
import functools

import jax
import jax.numpy as jnp
from jax import lax
from jax.experimental import pallas as pl
from jax.experimental.pallas import tpu as pltpu
from jax.sharding import PartitionSpec as P

MESH = pl.DeviceIdType.MESH
F32 = jnp.float32
BF16 = jnp.bfloat16
NZ, NX, NC, NY = 4, 4, 2, 4
PAIR = 20
TOP = 16
REST = PAIR - TOP
LINE = 4 * PAIR
LANES = 128
FAR = (2, 1, 3, 0)


def dot(a, b, ca=1, cb=0):
    return lax.dot_general(a, b, (((ca,), (cb,)), ((), ())), preferred_element_type=F32)


def kernel(
    counts_ref, ids_ref, codes_ref, route_ref, tok_ref, cot_ref, comp_ref, wg_hbm, wu_hbm, wd_hbm,
    layer_ref, grad_ref, down_hbm, mid_a0, mid_a1, mid_b0, mid_b1, mid_c0, mid_c1, mid_d0, mid_d1,
    send_0, send_1, got_a, got_b, got_c, got_d, wg, wu, wd, rows, gate, up, hid, dgs, dus,
    part, relay, final, mix_out, mix_in, loc_out, loc_in, wsem, osem, ss1, rs1, ss2, rs2, yss, yrs,
):
    devs = NZ * NX * NC
    top_rows, all_rows = devs * TOP, devs * PAIR
    tok_n, width = tok_ref.shape
    quarter = width // 4
    ff = wg.shape[2]
    me, y = lax.axis_index("expert"), lax.axis_index("dp")
    c, x, z = me % NC, (me // NC) % NX, me // (NC * NX)

    def at(zz, xx, cc):
        return {"expert": (zz * NX + xx) * NC + cc}

    def x_dev(dx, dc, back=False):
        return at(z, (x + (NX - dx if back else dx)) % NX, (c + dc) % NC)

    def z_dev(dz, dc, back=False):
        return at((z + (NZ - dz if back else dz)) % NZ, x, (c + dc) % NC)

    def y_dev(dy):
        return {"dp": (y + dy) % NY}

    peers = [x_dev(d, k) for d in range(NX) for k in range(NC) if d + k]
    peers += [z_dev(d, k) for d in range(1, NZ) for k in range(NC)]
    peers += [y_dev(1), y_dev(NY - 1)]
    barrier = pltpu.get_barrier_semaphore()
    for peer in peers:
        pl.semaphore_signal(barrier, inc=1, device_id=peer, device_id_type=MESH)

    loads = [
        pltpu.make_async_copy(src, dst, wsem.at[i])
        for i, (src, dst) in enumerate(((wg_hbm, wg), (wu_hbm, wu), (wd_hbm, wd)))
    ]
    for load in loads:
        load.start()

    sends = (send_0, send_1, send_0, send_1)
    mids = ((mid_a0, mid_a1), (mid_b0, mid_b1), (mid_c0, mid_c1), (mid_d0, mid_d1))
    gots = (got_a, got_b, got_c, got_d)

    def copies(n, phase):
        out = ([], [])
        buf, (mid_x, mid_z), got = sends[n], mids[n], gots[n]
        ssem, rsem = ((ss1, rs1), (ss2, rs2))[phase]
        for d in FAR:
            for k in (1, 0):
                cc = (c + k) % NC
                xx, zz = (x + d) % NX, (z + d) % NZ
                if phase == 0:
                    moves = (
                        (buf.at[cc, :, xx], mid_x.at[x, c], x_dev(d, k)),
                        (buf.at[NC + cc, zz], mid_z.at[z, c], z_dev(d, k)),
                    )
                else:
                    moves = (
                        (mid_z.at[:, :, xx, cc], got.at[NC + c, :, x], x_dev(d, k)),
                        (mid_x.at[:, :, zz, cc], got.at[c, z], z_dev(d, k)),
                    )
                for side, (src, dst, dev) in enumerate(moves):
                    i = d * NC + k
                    if d + k:
                        out[side].append(functools.partial(
                            pltpu.make_async_remote_copy, src_ref=src, dst_ref=dst,
                            send_sem=ssem.at[n, side, i], recv_sem=rsem.at[n, side, i],
                            device_id=dev, device_id_type=MESH,
                        ))
                    else:
                        out[side].append(functools.partial(
                            pltpu.make_async_copy, src, dst, rsem.at[n, side, i]
                        ))
        return out

    def start(n, phase, sides=(0, 1)):
        both = copies(n, phase)
        for i in range(len(both[0])):
            for side in sides:
                both[side][i]().start()

    def arrive(n, phase, sides=(0, 1)):
        both = copies(n, phase)
        for side in sides:
            for copy in both[side][:-1]:
                copy().wait_recv()
            both[side][-1]().wait()

    def sent(n, phase):
        for side in copies(n, phase):
            for copy in side[:-1]:
                copy().wait_send()

    def relay_on(n):
        arrive(n, 0, (0,))
        start(n, 1, (1,))
        arrive(n, 0, (1,))
        start(n, 1, (0,))

    def pick(q, rows_n, cols_n, flip):
        i = lax.broadcasted_iota(jnp.int32, (rows_n, cols_n), 1 if flip else 0)
        j = lax.broadcasted_iota(jnp.int32, (rows_n, cols_n), 0 if flip else 1)
        return (j == (i // REST) * TOP + q * REST + i % REST).astype(F32).astype(BF16)

    def put_rows(n, q, value):
        buf = sends[n]
        rest = dot(pick(q, top_rows, devs * REST, True), value[top_rows:])
        line = lax.broadcasted_iota(jnp.int32, (top_rows, 1), 0) % TOP // REST
        at_q = pl.ds(pl.multiple_of(q * TOP, TOP), TOP)
        for g in range(4):
            cut = slice(g * LANES, (g + 1) * LANES)
            buf[g, :, :, :, at_q, :] = value[:top_rows, cut].reshape(NZ, NX, NC, TOP, LANES)
            old = buf[g, :, :, :, 4 * TOP:, :].reshape(top_rows, LANES)
            new = jnp.where(line == q, rest[:, cut], old.astype(F32)).astype(BF16)
            buf[g, :, :, :, 4 * TOP:, :] = new.reshape(NZ, NX, NC, TOP, LANES)

    def take_rows(n):
        got = gots[n]

        def body(q, carry):
            at_q = pl.ds(pl.multiple_of(q * TOP, TOP), TOP)
            col = pl.multiple_of(q * quarter, quarter)
            sel = pick(q, devs * REST, top_rows, False)
            for g in range(4):
                lanes = pl.ds(pl.multiple_of(col + g * LANES, LANES), LANES)
                rows[:top_rows, lanes] = got[g, :, :, :, at_q, :].reshape(top_rows, LANES)
            rest = jnp.concatenate(
                [got[g, :, :, :, 4 * TOP:, :].reshape(top_rows, LANES) for g in range(4)], axis=1
            )
            rows[top_rows:, pl.ds(col, quarter)] = dot(sel, rest).astype(BF16)
            return carry

        lax.fori_loop(0, 4, body, 0)

    ids, codes, route = ids_ref[...], codes_ref[...], route_ref[...]
    experts = 2 * devs
    size = jnp.ones_like(ids)
    base = jnp.zeros_like(ids)
    for e in range(experts):
        hit = ids == e
        size = jnp.where(hit, counts_ref[e], size)
        if e % 2:
            base = jnp.where(hit, counts_ref[e - 1], base)
    code_f, size_f = codes.astype(F32), size.astype(F32)
    bucket = base + codes - jnp.floor((code_f + 0.5) / size_f).astype(jnp.int32) * size
    dest = ids // 2
    row_id = jnp.where(bucket < TOP, dest * TOP + bucket, top_rows + dest * REST + bucket - TOP)
    row_iota = lax.broadcasted_iota(jnp.int32, (all_rows, tok_n), 0)
    member = jnp.zeros((all_rows, tok_n), F32)
    weight = jnp.zeros((all_rows, tok_n), F32)
    e_iota = lax.broadcasted_iota(jnp.int32, (experts, tok_n), 0)
    gain = jnp.zeros((experts, tok_n), F32)
    for k in range(ids.shape[0]):
        hit = row_iota == row_id[k:k + 1, :]
        member = jnp.where(hit, 1.0, member)
        weight = jnp.where(hit, route[k:k + 1, :], weight)
        gain = jnp.where(e_iota == ids[k:k + 1, :], route[k:k + 1, :], gain)
    inverse = 1.0 / jnp.maximum(jnp.sum(member, axis=1, keepdims=True), 1.0)
    member_b, weight_b = member.astype(BF16), weight.astype(BF16)
    mix_out[...] = weight.T.astype(BF16)
    mix_in[...] = (member * inverse).T.astype(BF16)
    gain_b = gain.T.astype(BF16)

    row_e = lax.broadcasted_iota(jnp.int32, (all_rows, experts), 0)
    col_e = lax.broadcasted_iota(jnp.int32, (all_rows, experts), 1)
    row_dest = jnp.where(row_e < top_rows, row_e // TOP, (row_e - top_rows) // REST)
    row_bucket = jnp.where(row_e < top_rows, row_e % TOP, TOP)
    first = lax.broadcasted_iota(jnp.int32, (1, experts), 1)
    first_n = jnp.zeros((1, experts), jnp.int32)
    for j in range(devs):
        first_n = jnp.where(first // 2 == j, counts_ref[2 * j], first_n)
    owner = jnp.where(
        (col_e // 2 == row_dest) & ((row_bucket >= first_n) == (col_e % 2 == 1)), 1.0, 0.0
    ).astype(BF16)

    def head(n, lhs, scale, src, mix, loc):
        def sums(q, carry):
            cols = pl.ds(pl.multiple_of(q * quarter, quarter), quarter)
            value = dot(lhs, src[:, cols])
            if scale is not None:
                value = value * scale
            value = value.astype(BF16)
            rows[:, cols] = value
            put_rows(n, q, value)
            return carry

        lax.fori_loop(0, 4, sums, 0)
        if n == 0:
            pl.semaphore_wait(barrier, len(peers))
        start(n, 0)

        def local(q, carry):
            cols = pl.ds(pl.multiple_of(q * quarter, quarter), quarter)
            comp = comp_ref[:, cols]
            scaled = (dot(owner, comp) * rows[:, cols].astype(F32)).astype(BF16)
            loc[:, cols] = dot(gain_b, comp) * src[:, cols].astype(F32) - dot(mix[...], scaled)
            return carry

        lax.fori_loop(0, 4, local, 0)

    for ref in (send_0, send_1):
        ref[:, :, :, :, 4 * TOP:, :] = jnp.zeros((4, NZ, NX, NC, TOP, LANES), BF16)
    head(0, member_b, inverse, tok_ref, mix_out, loc_out)
    head(1, weight_b, None, cot_ref, mix_in, loc_in)
    relay_on(0)
    relay_on(1)
    sent(0, 0)
    for load in loads:
        load.wait()

    mine = counts_ref[2 * me]
    row_1 = lax.broadcasted_iota(jnp.int32, (all_rows, 1), 0)
    zero_exp = (row_1 < top_rows) & (row_1 % TOP < mine)
    step = 256
    arrive(0, 1)
    take_rows(0)

    def both(w, cols):
        return jnp.where(zero_exp, dot(rows[...], w[0, :, cols]), dot(rows[...], w[1, :, cols]))

    def split(ref, f, value):
        ref[:, pl.ds(f, step)] = jnp.where(zero_exp, value, 0.0).astype(BF16)
        ref[:, pl.ds(pl.multiple_of(f + ff, step), step)] = jnp.where(zero_exp, 0.0, value).astype(BF16)

    def forward(i, carry):
        f = pl.multiple_of(i * step, step)
        cols = pl.ds(f, step)
        g, u = both(wg, cols), both(wu, cols)
        gate[:, cols] = g.astype(BF16)
        up[:, cols] = u.astype(BF16)
        split(hid, f, g * jax.nn.sigmoid(g) * u)
        return carry

    lax.fori_loop(0, ff // step, forward, 0)

    def out_cols(q, carry):
        cols = pl.ds(pl.multiple_of(q * quarter, quarter), quarter)
        put_rows(2, q, dot(hid[...], wd[:, cols]).astype(BF16))
        return carry

    lax.fori_loop(0, 4, out_cols, 0)
    start(2, 0)

    arrive(1, 1)
    sent(1, 0)
    take_rows(1)

    def y_copy(i):
        e, dest, sign, dst = (
            (0, 2, 1, relay.at[0]), (1, 2, NY - 1, relay.at[1]),
            (1, 1, 1, final.at[0, 1]), (0, NY - 1, NY - 1, final.at[1, 0]),
            (0, 1, 1, final.at[0, 0]), (1, NY - 1, NY - 1, final.at[1, 1]),
        )[i]
        return pltpu.make_async_remote_copy(
            src_ref=part.at[(y + dest) % NY, e], dst_ref=dst, send_sem=yss.at[i],
            recv_sem=yrs.at[i], device_id=y_dev(sign), device_id_type=MESH,
        )

    def down(shift):
        owner_y = (y + shift) % NY
        cols = pl.ds(pl.multiple_of(owner_y * quarter, quarter), quarter)

        def body(i, carry):
            f = pl.multiple_of(i * step, step)
            for e in range(2):
                at_f = pl.ds(pl.multiple_of(f + e * ff, step), step)
                part[owner_y, e, pl.ds(f, step), :] = dot(hid[:, at_f], rows[:, cols], 0, 0).astype(BF16)
            return carry

        lax.fori_loop(0, ff // step, body, 0)

    down(2)
    y_copy(0).start()
    y_copy(1).start()
    down(1)
    y_copy(2).start()
    down(NY - 1)
    y_copy(3).start()
    down(0)

    def backward(i, carry):
        f = pl.multiple_of(i * step, step)
        cols = pl.ds(f, step)
        high = pl.ds(pl.multiple_of(f + ff, step), step)
        dh = jnp.where(zero_exp, dot(rows[...], wd[cols, :], 1, 1), dot(rows[...], wd[high, :], 1, 1))
        g, u = gate[:, cols].astype(F32), up[:, cols].astype(F32)
        s = jax.nn.sigmoid(g)
        split(dgs, f, dh * u * s * (1.0 + g * (1.0 - s)))
        split(dus, f, dh * g * s)
        return carry

    lax.fori_loop(0, ff // step, backward, 0)
    relay_on(2)

    def back_cols(q, carry):
        at_q = pl.ds(pl.multiple_of(q * quarter, quarter), quarter)
        total = jnp.zeros((all_rows, quarter), F32)
        for e in range(2):
            half = slice(e * ff, (e + 1) * ff)
            total += dot(dgs[:, half], wg[e, at_q, :], 1, 1)
            total += dot(dus[:, half], wu[e, at_q, :], 1, 1)
        put_rows(3, q, total.astype(BF16))
        return carry

    lax.fori_loop(0, 4, back_cols, 0)
    start(3, 0)

    for i, shift, e in ((0, 1, 0), (1, NY - 1, 1)):
        y_copy(i).wait_recv()
        owner_y = (y + shift) % NY

        def add(j, carry):
            at_f = pl.ds(pl.multiple_of(j * step, step), step)
            total = part[owner_y, e, at_f, :].astype(F32) + relay[i, at_f, :].astype(F32)
            part[owner_y, e, at_f, :] = total.astype(BF16)
            return carry

        lax.fori_loop(0, ff // step, add, 0)
        y_copy(4 + i).start()
    relay_on(3)

    def tail(n, mix, loc, out_ref):
        arrive(n, 1)
        take_rows(n)

        def body(q, carry):
            cols = pl.ds(pl.multiple_of(q * quarter, quarter), quarter)
            out_ref[:, cols] = (loc[:, cols] + dot(mix[...], rows[:, cols])).astype(BF16)
            return carry

        lax.fori_loop(0, 4, body, 0)

    tail(2, mix_out, loc_out, layer_ref)
    for i in range(2, 6):
        y_copy(i).wait_recv()

    def finish(j, carry):
        at_f = pl.ds(pl.multiple_of(j * step, step), step)
        for e in range(2):
            total = part[y, e, at_f, :].astype(F32) + final[0, e, at_f, :].astype(F32)
            relay[e, at_f, :] = (total + final[1, e, at_f, :].astype(F32)).astype(BF16)
        return carry

    lax.fori_loop(0, ff // step, finish, 0)
    down_out = pltpu.make_async_copy(relay, down_hbm, osem)
    down_out.start()
    tail(3, mix_in, loc_in, grad_ref)
    for n in range(4):
        if n >= 2:
            sent(n, 0)
        sent(n, 1)
    for i in range(6):
        y_copy(i).wait_send()
    down_out.wait()


def on_device(
    tokens, expert_ids, bucket_codes, route_weights, cotangent, counts, comp_scale, w_gate, w_up, w_down
):
    tok_n, width = tokens.shape
    local, _, ff = w_gate.shape
    devs = NZ * NX * NC
    all_rows, quarter = devs * PAIR, width // 4
    vmem = pl.BlockSpec(memory_space=pltpu.VMEM)
    hbm = pl.BlockSpec(memory_space=pl.ANY)
    mid = jax.ShapeDtypeStruct((4, NC, 4, NC, LINE, LANES), BF16)
    rows_buf = pltpu.VMEM((4, NZ, NX, NC, LINE, LANES), BF16)
    dma = pltpu.SemaphoreType.DMA
    out = pl.pallas_call(
        kernel,
        out_shape=[
            jax.ShapeDtypeStruct((tok_n, width), BF16),
            jax.ShapeDtypeStruct((tok_n, width), BF16),
            jax.ShapeDtypeStruct((local, ff, quarter), BF16),
        ] + [mid] * 8,
        in_specs=[pl.BlockSpec(memory_space=pltpu.SMEM)] + [vmem] * 6 + [hbm] * 3,
        out_specs=[vmem] * 2 + [hbm] * 9,
        scratch_shapes=[rows_buf] * 6 + [
            pltpu.VMEM((local, width, ff), BF16),
            pltpu.VMEM((local, width, ff), BF16),
            pltpu.VMEM((local * ff, width), BF16),
            pltpu.VMEM((all_rows, width), BF16),
            pltpu.VMEM((all_rows, ff), BF16),
            pltpu.VMEM((all_rows, ff), BF16),
            pltpu.VMEM((all_rows, local * ff), BF16),
            pltpu.VMEM((all_rows, local * ff), BF16),
            pltpu.VMEM((all_rows, local * ff), BF16),
            pltpu.VMEM((NY, local, ff, quarter), BF16),
            pltpu.VMEM((2, ff, quarter), BF16),
            pltpu.VMEM((2, local, ff, quarter), BF16),
            pltpu.VMEM((tok_n, all_rows), BF16),
            pltpu.VMEM((tok_n, all_rows), BF16),
            pltpu.VMEM((tok_n, width), F32),
            pltpu.VMEM((tok_n, width), F32),
            dma((3,)), dma, dma((4, 2, 8)), dma((4, 2, 8)), dma((4, 2, 8)), dma((4, 2, 8)),
            dma((6,)), dma((6,)),
        ],
        compiler_params=pltpu.CompilerParams(
            collective_id=0, has_side_effects=True, vmem_limit_bytes=67043328
        ),
    )(
        counts, expert_ids.T, bucket_codes.T, route_weights.T, tokens, cotangent, comp_scale,
        w_gate, w_up, w_down.reshape(local * ff, width),
    )
    return tuple(out[:3])


def solution(mesh):
    rows = P(("dp", "expert"), None)
    stack = P("expert", None, None)
    return jax.shard_map(
        on_device,
        mesh=mesh,
        in_specs=(rows, rows, rows, rows, rows, P(), P(), stack, stack, stack),
        out_specs=(rows, rows, P("expert", None, "dp")),
        check_vma=False,
    )
```

```python
import functools

import jax
import jax.numpy as jnp
from jax import lax
from jax.experimental import pallas as pl
from jax.experimental.pallas import tpu as pltpu
from jax.sharding import PartitionSpec as P

MESH = pl.DeviceIdType.MESH
F32 = jnp.float32
BF16 = jnp.bfloat16
NZ, NX, NC, NY = 4, 4, 2, 4
PAIR = 20
TOP = 16
REST = PAIR - TOP
LINE = 4 * PAIR
LANES = 128
FAR = (2, 1, 3, 0)


def dot(a, b, ca=1, cb=0):
    return lax.dot_general(a, b, (((ca,), (cb,)), ((), ())), preferred_element_type=F32)


def kernel(
    counts_ref, ids_ref, codes_ref, route_ref, tok_ref, cot_ref, comp_ref, wg_hbm, wu_hbm, wd_hbm,
    layer_ref, grad_ref, down_hbm, mid_a0, mid_a1, mid_b0, mid_b1, mid_c0, mid_c1, mid_d0, mid_d1,
    send_0, send_1, got_a, got_b, got_c, got_d, wg, wu, wd, rows, gate, up, hid, dgs, dus,
    part, relay, final, mix_out, mix_in, loc_out, loc_in, wsem, osem, ss1, rs1, ss2, rs2, yss, yrs,
):
    devs = NZ * NX * NC
    top_rows, all_rows = devs * TOP, devs * PAIR
    tok_n, width = tok_ref.shape
    quarter = width // 4
    ff = wg.shape[2]
    me, y = lax.axis_index("expert"), lax.axis_index("dp")
    c, x, z = me % NC, (me // NC) % NX, me // (NC * NX)

    def at(zz, xx, cc):
        return {"expert": (zz * NX + xx) * NC + cc}

    def x_dev(dx, dc, back=False):
        return at(z, (x + (NX - dx if back else dx)) % NX, (c + dc) % NC)

    def z_dev(dz, dc, back=False):
        return at((z + (NZ - dz if back else dz)) % NZ, x, (c + dc) % NC)

    def y_dev(dy):
        return {"dp": (y + dy) % NY}

    peers = [x_dev(d, k) for d in range(NX) for k in range(NC) if d + k]
    peers += [z_dev(d, k) for d in range(1, NZ) for k in range(NC)]
    peers += [y_dev(1), y_dev(NY - 1)]
    barrier = pltpu.get_barrier_semaphore()
    for peer in peers:
        pl.semaphore_signal(barrier, inc=1, device_id=peer, device_id_type=MESH)

    loads = [
        pltpu.make_async_copy(src, dst, wsem.at[i])
        for i, (src, dst) in enumerate(((wg_hbm, wg), (wu_hbm, wu), (wd_hbm, wd)))
    ]
    for load in loads:
        load.start()

    sends = (send_0, send_1, send_0, send_1)
    mids = ((mid_a0, mid_a1), (mid_b0, mid_b1), (mid_c0, mid_c1), (mid_d0, mid_d1))
    gots = (got_a, got_b, got_c, got_d)

    def copies(n, phase):
        out = ([], [])
        buf, (mid_x, mid_z), got = sends[n], mids[n], gots[n]
        ssem, rsem = ((ss1, rs1), (ss2, rs2))[phase]
        for d in FAR:
            for k in (1, 0):
                cc = (c + k) % NC
                xx, zz = (x + d) % NX, (z + d) % NZ
                if phase == 0:
                    moves = (
                        (buf.at[cc, :, xx], mid_x.at[x, c], x_dev(d, k)),
                        (buf.at[NC + cc, zz], mid_z.at[z, c], z_dev(d, k)),
                    )
                else:
                    moves = (
                        (mid_z.at[:, :, xx, cc], got.at[NC + c, :, x], x_dev(d, k)),
                        (mid_x.at[:, :, zz, cc], got.at[c, z], z_dev(d, k)),
                    )
                for side, (src, dst, dev) in enumerate(moves):
                    i = d * NC + k
                    if d + k:
                        out[side].append(functools.partial(
                            pltpu.make_async_remote_copy, src_ref=src, dst_ref=dst,
                            send_sem=ssem.at[n, side, i], recv_sem=rsem.at[n, side, i],
                            device_id=dev, device_id_type=MESH,
                        ))
                    else:
                        out[side].append(functools.partial(
                            pltpu.make_async_copy, src, dst, rsem.at[n, side, i]
                        ))
        return out

    def start(n, phase, sides=(0, 1)):
        both = copies(n, phase)
        for i in range(len(both[0])):
            for side in sides:
                both[side][i]().start()

    def arrive(n, phase, sides=(0, 1)):
        both = copies(n, phase)
        for side in sides:
            for copy in both[side][:-1]:
                copy().wait_recv()
            both[side][-1]().wait()

    def sent(n, phase):
        for side in copies(n, phase):
            for copy in side[:-1]:
                copy().wait_send()

    def relay_on(n):
        arrive(n, 0, (0,))
        start(n, 1, (1,))
        arrive(n, 0, (1,))
        start(n, 1, (0,))

    def pick(q, rows_n, cols_n, flip):
        i = lax.broadcasted_iota(jnp.int32, (rows_n, cols_n), 1 if flip else 0)
        j = lax.broadcasted_iota(jnp.int32, (rows_n, cols_n), 0 if flip else 1)
        return (j == (i // REST) * TOP + q * REST + i % REST).astype(F32).astype(BF16)

    def put_rows(n, q, value):
        buf = sends[n]
        rest = dot(pick(q, top_rows, devs * REST, True), value[top_rows:])
        line = lax.broadcasted_iota(jnp.int32, (top_rows, 1), 0) % TOP // REST
        at_q = pl.ds(pl.multiple_of(q * TOP, TOP), TOP)
        for g in range(4):
            cut = slice(g * LANES, (g + 1) * LANES)
            buf[g, :, :, :, at_q, :] = value[:top_rows, cut].reshape(NZ, NX, NC, TOP, LANES)
            old = buf[g, :, :, :, 4 * TOP:, :].reshape(top_rows, LANES)
            new = jnp.where(line == q, rest[:, cut], old.astype(F32)).astype(BF16)
            buf[g, :, :, :, 4 * TOP:, :] = new.reshape(NZ, NX, NC, TOP, LANES)

    def take_rows(n):
        got = gots[n]

        def body(q, carry):
            at_q = pl.ds(pl.multiple_of(q * TOP, TOP), TOP)
            col = pl.multiple_of(q * quarter, quarter)
            sel = pick(q, devs * REST, top_rows, False)
            for g in range(4):
                lanes = pl.ds(pl.multiple_of(col + g * LANES, LANES), LANES)
                rows[:top_rows, lanes] = got[g, :, :, :, at_q, :].reshape(top_rows, LANES)
            rest = jnp.concatenate(
                [got[g, :, :, :, 4 * TOP:, :].reshape(top_rows, LANES) for g in range(4)], axis=1
            )
            rows[top_rows:, pl.ds(col, quarter)] = dot(sel, rest).astype(BF16)
            return carry

        lax.fori_loop(0, 4, body, 0)

    ids, codes, route = ids_ref[...], codes_ref[...], route_ref[...]
    experts = 2 * devs
    size = jnp.ones_like(ids)
    base = jnp.zeros_like(ids)
    for e in range(experts):
        hit = ids == e
        size = jnp.where(hit, counts_ref[e], size)
        if e % 2:
            base = jnp.where(hit, counts_ref[e - 1], base)
    code_f, size_f = codes.astype(F32), size.astype(F32)
    bucket = base + codes - jnp.floor((code_f + 0.5) / size_f).astype(jnp.int32) * size
    dest = ids // 2
    row_id = jnp.where(bucket < TOP, dest * TOP + bucket, top_rows + dest * REST + bucket - TOP)
    row_iota = lax.broadcasted_iota(jnp.int32, (all_rows, tok_n), 0)
    member = jnp.zeros((all_rows, tok_n), F32)
    weight = jnp.zeros((all_rows, tok_n), F32)
    e_iota = lax.broadcasted_iota(jnp.int32, (experts, tok_n), 0)
    gain = jnp.zeros((experts, tok_n), F32)
    for k in range(ids.shape[0]):
        hit = row_iota == row_id[k:k + 1, :]
        member = jnp.where(hit, 1.0, member)
        weight = jnp.where(hit, route[k:k + 1, :], weight)
        gain = jnp.where(e_iota == ids[k:k + 1, :], route[k:k + 1, :], gain)
    inverse = 1.0 / jnp.maximum(jnp.sum(member, axis=1, keepdims=True), 1.0)
    member_b, weight_b = member.astype(BF16), weight.astype(BF16)
    mix_out[...] = weight.T.astype(BF16)
    mix_in[...] = (member * inverse).T.astype(BF16)
    gain_b = gain.T.astype(BF16)

    row_e = lax.broadcasted_iota(jnp.int32, (all_rows, experts), 0)
    col_e = lax.broadcasted_iota(jnp.int32, (all_rows, experts), 1)
    row_dest = jnp.where(row_e < top_rows, row_e // TOP, (row_e - top_rows) // REST)
    row_bucket = jnp.where(row_e < top_rows, row_e % TOP, TOP)
    first = lax.broadcasted_iota(jnp.int32, (1, experts), 1)
    first_n = jnp.zeros((1, experts), jnp.int32)
    for j in range(devs):
        first_n = jnp.where(first // 2 == j, counts_ref[2 * j], first_n)
    owner = jnp.where(
        (col_e // 2 == row_dest) & ((row_bucket >= first_n) == (col_e % 2 == 1)), 1.0, 0.0
    ).astype(BF16)

    def head(n, lhs, scale, src, mix, loc):
        def sums(q, carry):
            cols = pl.ds(pl.multiple_of(q * quarter, quarter), quarter)
            value = dot(lhs, src[:, cols])
            if scale is not None:
                value = value * scale
            value = value.astype(BF16)
            rows[:, cols] = value
            put_rows(n, q, value)
            return carry

        lax.fori_loop(0, 4, sums, 0)
        if n == 0:
            pl.semaphore_wait(barrier, len(peers))
            start(n, 0)

        def local(q, carry):
            cols = pl.ds(pl.multiple_of(q * quarter, quarter), quarter)
            comp = comp_ref[:, cols]
            scaled = (dot(owner, comp) * rows[:, cols].astype(F32)).astype(BF16)
            loc[:, cols] = dot(gain_b, comp) * src[:, cols].astype(F32) - dot(mix[...], scaled)
            return carry

        lax.fori_loop(0, 4, local, 0)

    for ref in (send_0, send_1):
        ref[:, :, :, :, 4 * TOP:, :] = jnp.zeros((4, NZ, NX, NC, TOP, LANES), BF16)
    head(0, member_b, inverse, tok_ref, mix_out, loc_out)
    head(1, weight_b, None, cot_ref, mix_in, loc_in)
    relay_on(0)
    start(1, 0)
    sent(0, 0)
    for load in loads:
        load.wait()

    mine = counts_ref[2 * me]
    row_1 = lax.broadcasted_iota(jnp.int32, (all_rows, 1), 0)
    zero_exp = (row_1 < top_rows) & (row_1 % TOP < mine)
    step = 256
    arrive(0, 1)
    take_rows(0)

    def both(w, cols):
        return jnp.where(zero_exp, dot(rows[...], w[0, :, cols]), dot(rows[...], w[1, :, cols]))

    def split(ref, f, value):
        ref[:, pl.ds(f, step)] = jnp.where(zero_exp, value, 0.0).astype(BF16)
        ref[:, pl.ds(pl.multiple_of(f + ff, step), step)] = jnp.where(zero_exp, 0.0, value).astype(BF16)

    def forward(i, carry):
        f = pl.multiple_of(i * step, step)
        cols = pl.ds(f, step)
        g, u = both(wg, cols), both(wu, cols)
        gate[:, cols] = g.astype(BF16)
        up[:, cols] = u.astype(BF16)
        split(hid, f, g * jax.nn.sigmoid(g) * u)
        return carry

    lax.fori_loop(0, ff // step, forward, 0)
    relay_on(1)

    def out_cols(q, carry):
        cols = pl.ds(pl.multiple_of(q * quarter, quarter), quarter)
        put_rows(2, q, dot(hid[...], wd[:, cols]).astype(BF16))
        return carry

    lax.fori_loop(0, 4, out_cols, 0)
    start(2, 0)

    arrive(1, 1)
    sent(1, 0)
    take_rows(1)

    def y_copy(i):
        e, dest, sign, dst = (
            (0, 2, 1, relay.at[0]), (1, 2, NY - 1, relay.at[1]),
            (1, 1, 1, final.at[0, 1]), (0, NY - 1, NY - 1, final.at[1, 0]),
            (0, 1, 1, final.at[0, 0]), (1, NY - 1, NY - 1, final.at[1, 1]),
        )[i]
        return pltpu.make_async_remote_copy(
            src_ref=part.at[(y + dest) % NY, e], dst_ref=dst, send_sem=yss.at[i],
            recv_sem=yrs.at[i], device_id=y_dev(sign), device_id_type=MESH,
        )

    def down(shift):
        owner_y = (y + shift) % NY
        cols = pl.ds(pl.multiple_of(owner_y * quarter, quarter), quarter)

        def body(i, carry):
            f = pl.multiple_of(i * step, step)
            for e in range(2):
                at_f = pl.ds(pl.multiple_of(f + e * ff, step), step)
                part[owner_y, e, pl.ds(f, step), :] = dot(hid[:, at_f], rows[:, cols], 0, 0).astype(BF16)
            return carry

        lax.fori_loop(0, ff // step, body, 0)

    down(2)
    y_copy(0).start()
    y_copy(1).start()
    down(1)
    y_copy(2).start()
    down(NY - 1)
    y_copy(3).start()
    down(0)

    def backward(i, carry):
        f = pl.multiple_of(i * step, step)
        cols = pl.ds(f, step)
        high = pl.ds(pl.multiple_of(f + ff, step), step)
        dh = jnp.where(zero_exp, dot(rows[...], wd[cols, :], 1, 1), dot(rows[...], wd[high, :], 1, 1))
        g, u = gate[:, cols].astype(F32), up[:, cols].astype(F32)
        s = jax.nn.sigmoid(g)
        split(dgs, f, dh * u * s * (1.0 + g * (1.0 - s)))
        split(dus, f, dh * g * s)
        return carry

    lax.fori_loop(0, ff // step, backward, 0)
    relay_on(2)

    def back_cols(q, carry):
        at_q = pl.ds(pl.multiple_of(q * quarter, quarter), quarter)
        total = jnp.zeros((all_rows, quarter), F32)
        for e in range(2):
            half = slice(e * ff, (e + 1) * ff)
            total += dot(dgs[:, half], wg[e, at_q, :], 1, 1)
            total += dot(dus[:, half], wu[e, at_q, :], 1, 1)
        put_rows(3, q, total.astype(BF16))
        return carry

    lax.fori_loop(0, 4, back_cols, 0)
    start(3, 0)

    for i, shift, e in ((0, 1, 0), (1, NY - 1, 1)):
        y_copy(i).wait_recv()
        owner_y = (y + shift) % NY

        def add(j, carry):
            at_f = pl.ds(pl.multiple_of(j * step, step), step)
            total = part[owner_y, e, at_f, :].astype(F32) + relay[i, at_f, :].astype(F32)
            part[owner_y, e, at_f, :] = total.astype(BF16)
            return carry

        lax.fori_loop(0, ff // step, add, 0)
        y_copy(4 + i).start()
    relay_on(3)

    def tail(n, mix, loc, out_ref):
        arrive(n, 1)
        take_rows(n)

        def body(q, carry):
            cols = pl.ds(pl.multiple_of(q * quarter, quarter), quarter)
            out_ref[:, cols] = (loc[:, cols] + dot(mix[...], rows[:, cols])).astype(BF16)
            return carry

        lax.fori_loop(0, 4, body, 0)

    tail(2, mix_out, loc_out, layer_ref)
    for i in range(2, 6):
        y_copy(i).wait_recv()

    def finish(j, carry):
        at_f = pl.ds(pl.multiple_of(j * step, step), step)
        for e in range(2):
            total = part[y, e, at_f, :].astype(F32) + final[0, e, at_f, :].astype(F32)
            relay[e, at_f, :] = (total + final[1, e, at_f, :].astype(F32)).astype(BF16)
        return carry

    lax.fori_loop(0, ff // step, finish, 0)
    down_out = pltpu.make_async_copy(relay, down_hbm, osem)
    down_out.start()
    tail(3, mix_in, loc_in, grad_ref)
    for n in range(4):
        if n >= 2:
            sent(n, 0)
        sent(n, 1)
    for i in range(6):
        y_copy(i).wait_send()
    down_out.wait()


def ship(*refs):
    count = (len(refs) - 2) // 3
    srcs, dsts, bufs = (refs[i * count:(i + 1) * count] for i in range(3))
    in_sem, out_sem = refs[3 * count:]
    reads = [pltpu.make_async_copy(s, b, in_sem.at[i]) for i, (s, b) in enumerate(zip(srcs, bufs))]
    writes = [pltpu.make_async_copy(b, d, out_sem.at[i]) for i, (b, d) in enumerate(zip(bufs, dsts))]
    for read in reads:
        read.start()
    for read, write in zip(reads, writes):
        read.wait()
        write.start()
    for write in writes:
        write.wait()


def on_device(
    tokens, expert_ids, bucket_codes, route_weights, cotangent, counts, comp_scale, w_gate, w_up, w_down
):
    tok_n, width = tokens.shape
    local, _, ff = w_gate.shape
    devs = NZ * NX * NC
    all_rows, quarter = devs * PAIR, width // 4
    vmem = pl.BlockSpec(memory_space=pltpu.VMEM)
    hbm = pl.BlockSpec(memory_space=pl.ANY)
    mid = jax.ShapeDtypeStruct((4, NC, 4, NC, LINE, LANES), BF16)
    rows_buf = pltpu.VMEM((4, NZ, NX, NC, LINE, LANES), BF16)
    dma = pltpu.SemaphoreType.DMA
    out = pl.pallas_call(
        kernel,
        out_shape=[
            jax.ShapeDtypeStruct((tok_n, width), BF16),
            jax.ShapeDtypeStruct((tok_n, width), BF16),
            jax.ShapeDtypeStruct((local, ff, quarter), BF16),
        ] + [mid] * 8,
        in_specs=[pl.BlockSpec(memory_space=pltpu.SMEM)] + [vmem] * 6 + [hbm] * 3,
        out_specs=[vmem] * 2 + [hbm] * 9,
        scratch_shapes=[rows_buf] * 6 + [
            pltpu.VMEM((local, width, ff), BF16),
            pltpu.VMEM((local, width, ff), BF16),
            pltpu.VMEM((local * ff, width), BF16),
            pltpu.VMEM((all_rows, width), BF16),
            pltpu.VMEM((all_rows, ff), BF16),
            pltpu.VMEM((all_rows, ff), BF16),
            pltpu.VMEM((all_rows, local * ff), BF16),
            pltpu.VMEM((all_rows, local * ff), BF16),
            pltpu.VMEM((all_rows, local * ff), BF16),
            pltpu.VMEM((NY, local, ff, quarter), BF16),
            pltpu.VMEM((2, ff, quarter), BF16),
            pltpu.VMEM((2, local, ff, quarter), BF16),
            pltpu.VMEM((tok_n, all_rows), BF16),
            pltpu.VMEM((tok_n, all_rows), BF16),
            pltpu.VMEM((tok_n, width), F32),
            pltpu.VMEM((tok_n, width), F32),
            dma((3,)), dma, dma((4, 2, 8)), dma((4, 2, 8)), dma((4, 2, 8)), dma((4, 2, 8)),
            dma((6,)), dma((6,)),
        ],
        compiler_params=pltpu.CompilerParams(
            collective_id=0, has_side_effects=True, vmem_limit_bytes=67043328
        ),
    )(
        counts, expert_ids.T, bucket_codes.T, route_weights.T, tokens, cotangent, comp_scale,
        w_gate, w_up, w_down.reshape(local * ff, width),
    )
    shapes = [jax.ShapeDtypeStruct(a.shape, a.dtype) for a in out[:3]]
    return tuple(pl.pallas_call(
        ship,
        out_shape=shapes,
        in_specs=[hbm] * 3,
        out_specs=[hbm] * 3,
        scratch_shapes=[pltpu.VMEM(a.shape, a.dtype) for a in shapes] + [dma((3,)), dma((3,))],
    )(*out[:3]))


def solution(mesh):
    rows = P(("dp", "expert"), None)
    stack = P("expert", None, None)
    return jax.shard_map(
        on_device,
        mesh=mesh,
        in_specs=(rows, rows, rows, rows, rows, P(), P(), stack, stack, stack),
        out_specs=(rows, rows, P("expert", None, "dp")),
        check_vma=False,
    )
```

```python
import functools

import jax
import jax.numpy as jnp
from jax import lax
from jax.experimental import pallas as pl
from jax.experimental.pallas import tpu as pltpu
from jax.sharding import PartitionSpec as P

MESH = pl.DeviceIdType.MESH
F32 = jnp.float32
BF16 = jnp.bfloat16
NZ, NX, NC, NY = 4, 4, 2, 4
PAIR = 20
TOP = 16
REST = PAIR - TOP
LINE = 4 * PAIR
LANES = 128
FAR = (2, 1, 3, 0)


def dot(a, b, ca=1, cb=0):
    return lax.dot_general(a, b, (((ca,), (cb,)), ((), ())), preferred_element_type=F32)


def kernel(
    counts_ref, ids_ref, codes_ref, route_ref, tok_ref, cot_ref, comp_ref, wg_hbm, wu_hbm, wd_hbm,
    layer_ref, grad_ref, down_hbm, mid_a0, mid_a1, mid_b0, mid_b1, mid_c0, mid_c1, mid_d0, mid_d1,
    send_0, send_1, got_a, got_b, got_c, got_d, wg, wu, wd, rows, spread, gate, up, hid, dgs, dus,
    part, relay, final, mix_out, mix_in, loc_out, loc_in, wsem, osem, ss1, rs1, ss2, rs2, yss, yrs,
):
    devs = NZ * NX * NC
    top_rows, all_rows = devs * TOP, devs * PAIR
    tok_n, width = tok_ref.shape
    quarter = width // 4
    ff = wg.shape[2]
    me, y = lax.axis_index("expert"), lax.axis_index("dp")
    c, x, z = me % NC, (me // NC) % NX, me // (NC * NX)

    def at(zz, xx, cc):
        return {"expert": (zz * NX + xx) * NC + cc}

    def x_dev(dx, dc, back=False):
        return at(z, (x + (NX - dx if back else dx)) % NX, (c + dc) % NC)

    def z_dev(dz, dc, back=False):
        return at((z + (NZ - dz if back else dz)) % NZ, x, (c + dc) % NC)

    def y_dev(dy):
        return {"dp": (y + dy) % NY}

    peers = [x_dev(d, k) for d in range(NX) for k in range(NC) if d + k]
    peers += [z_dev(d, k) for d in range(1, NZ) for k in range(NC)]
    peers += [y_dev(1), y_dev(NY - 1)]
    barrier = pltpu.get_barrier_semaphore()
    for peer in peers:
        pl.semaphore_signal(barrier, inc=1, device_id=peer, device_id_type=MESH)

    loads = [
        pltpu.make_async_copy(src, dst, wsem.at[i])
        for i, (src, dst) in enumerate(((wg_hbm, wg), (wu_hbm, wu), (wd_hbm, wd)))
    ]
    for load in loads:
        load.start()

    sends = (send_0, send_1, send_0, send_1)
    mids = ((mid_a0, mid_a1), (mid_b0, mid_b1), (mid_c0, mid_c1), (mid_d0, mid_d1))
    gots = (got_a, got_b, got_c, got_d)

    def move(n, phase, side, d, k, here):
        buf, (mid_x, mid_z), got = sends[n], mids[n], gots[n]
        ssem, rsem = ((ss1, rs1), (ss2, rs2))[phase]
        cc, xx, zz = (c + k) % NC, (x + d) % NX, (z + d) % NZ
        if phase == 0 and side == 0:
            src, dst = buf.at[cc, :, xx], mid_x.at[x, c]
        elif phase == 0:
            src, dst = buf.at[NC + cc, zz], mid_z.at[z, c]
        elif side == 0:
            src, dst = mid_z.at[:, :, xx, cc], got.at[NC + c, :, x]
        else:
            src, dst = mid_x.at[:, :, zz, cc], got.at[c, z]
        i = d * NC + k
        if here:
            return pltpu.make_async_copy(src, dst, rsem.at[n, side, i])
        return pltpu.make_async_remote_copy(
            src_ref=src, dst_ref=dst, send_sem=ssem.at[n, side, i], recv_sem=rsem.at[n, side, i],
            device_id=(z_dev if side else x_dev)(d, k), device_id_type=MESH,
        )

    def copies(n, phase):
        return [
            [functools.partial(move, n, phase, side, d, k, d + k == 0) for d in FAR for k in (1, 0)]
            for side in range(2)
        ]

    def start(n, phase, sides=(0, 1)):
        both = copies(n, phase)
        for i in range(len(both[0])):
            for side in sides:
                both[side][i]().start()

    def arrive(n, phase, sides=(0, 1)):
        both = copies(n, phase)
        for side in sides:
            for copy in both[side][:-1]:
                copy().wait_recv()
            both[side][-1]().wait()

    def sent(n, phase):
        for side in copies(n, phase):
            for copy in side[:-1]:
                copy().wait_send()

    def relay_on(n):
        arrive(n, 0, (0,))
        start(n, 1, (1,))
        arrive(n, 0, (1,))
        start(n, 1, (0,))

    def pick(q, rows_n, cols_n, flip):
        i = lax.broadcasted_iota(jnp.int32, (rows_n, cols_n), 1 if flip else 0)
        j = lax.broadcasted_iota(jnp.int32, (rows_n, cols_n), 0 if flip else 1)
        return (j == (i // REST) * TOP + q * REST + i % REST).astype(F32).astype(BF16)

    def lanes(g):
        return [pl.ds(pl.multiple_of(q * quarter + g * LANES, LANES), LANES) for q in range(4)]

    def send_groups(n, value_of):
        buf = sends[n]

        def body(j, carry):
            cc = (c + 1 - j) % NC
            for side in range(2):
                g = side * NC + cc
                value = value_of(g)
                cuts = [slice(q * LANES, (q + 1) * LANES) for q in range(4)]
                for q in range(4):
                    top = value[:top_rows, cuts[q]]
                    buf[g, :, :, :, q * TOP:(q + 1) * TOP, :] = top.reshape(NZ, NX, NC, TOP, LANES)
                rest = jnp.concatenate([value[top_rows:, cuts[q]] for q in range(4)], axis=0)
                rest = dot(spread[...], rest).astype(BF16)
                buf[g, :, :, :, 4 * TOP:, :] = rest.reshape(NZ, NX, NC, TOP, LANES)
                for d in FAR[:3]:
                    move(n, 0, side, d, 1 - j, False).start()

                @pl.when(j == 0)
                def _():
                    move(n, 0, side, 0, 1, False).start()

                @pl.when(j == 1)
                def _():
                    move(n, 0, side, 0, 0, True).start()
            return carry

        lax.fori_loop(0, NC, body, 0)

    def take_rows(n):
        got = gots[n]

        def body(q, carry):
            at_q = pl.ds(pl.multiple_of(q * TOP, TOP), TOP)
            col = pl.multiple_of(q * quarter, quarter)
            sel = pick(q, devs * REST, top_rows, False)
            for g in range(4):
                lanes = pl.ds(pl.multiple_of(col + g * LANES, LANES), LANES)
                rows[:top_rows, lanes] = got[g, :, :, :, at_q, :].reshape(top_rows, LANES)
            rest = jnp.concatenate(
                [got[g, :, :, :, 4 * TOP:, :].reshape(top_rows, LANES) for g in range(4)], axis=1
            )
            rows[top_rows:, pl.ds(col, quarter)] = dot(sel, rest).astype(BF16)
            return carry

        lax.fori_loop(0, 4, body, 0)

    ids, codes, route = ids_ref[...], codes_ref[...], route_ref[...]
    experts = 2 * devs
    size = jnp.ones_like(ids)
    base = jnp.zeros_like(ids)
    for e in range(experts):
        hit = ids == e
        size = jnp.where(hit, counts_ref[e], size)
        if e % 2:
            base = jnp.where(hit, counts_ref[e - 1], base)
    code_f, size_f = codes.astype(F32), size.astype(F32)
    bucket = base + codes - jnp.floor((code_f + 0.5) / size_f).astype(jnp.int32) * size
    dest = ids // 2
    row_id = jnp.where(bucket < TOP, dest * TOP + bucket, top_rows + dest * REST + bucket - TOP)
    row_iota = lax.broadcasted_iota(jnp.int32, (all_rows, tok_n), 0)
    member = jnp.zeros((all_rows, tok_n), F32)
    weight = jnp.zeros((all_rows, tok_n), F32)
    e_iota = lax.broadcasted_iota(jnp.int32, (experts, tok_n), 0)
    gain = jnp.zeros((experts, tok_n), F32)
    for k in range(ids.shape[0]):
        hit = row_iota == row_id[k:k + 1, :]
        member = jnp.where(hit, 1.0, member)
        weight = jnp.where(hit, route[k:k + 1, :], weight)
        gain = jnp.where(e_iota == ids[k:k + 1, :], route[k:k + 1, :], gain)
    inverse = 1.0 / jnp.maximum(jnp.sum(member, axis=1, keepdims=True), 1.0)
    member_b, weight_b = member.astype(BF16), weight.astype(BF16)
    mix_out[...] = weight.T.astype(BF16)
    mix_in[...] = (member * inverse).T.astype(BF16)
    gain_b = gain.T.astype(BF16)

    row_e = lax.broadcasted_iota(jnp.int32, (all_rows, experts), 0)
    col_e = lax.broadcasted_iota(jnp.int32, (all_rows, experts), 1)
    row_dest = jnp.where(row_e < top_rows, row_e // TOP, (row_e - top_rows) // REST)
    row_bucket = jnp.where(row_e < top_rows, row_e % TOP, TOP)
    first = lax.broadcasted_iota(jnp.int32, (1, experts), 1)
    first_n = jnp.zeros((1, experts), jnp.int32)
    for j in range(devs):
        first_n = jnp.where(first // 2 == j, counts_ref[2 * j], first_n)
    owner = jnp.where(
        (col_e // 2 == row_dest) & ((row_bucket >= first_n) == (col_e % 2 == 1)), 1.0, 0.0
    ).astype(BF16)

    def head(n, lhs, scale, src, mix, loc):
        def sums(g):
            value = dot(lhs, jnp.concatenate([src[:, cols] for cols in lanes(g)], axis=1))
            if scale is not None:
                value = value * scale
            value = value.astype(BF16)
            for q, cols in enumerate(lanes(g)):
                rows[:, cols] = value[:, q * LANES:(q + 1) * LANES]
            return value

        if n == 0:
            pl.semaphore_wait(barrier, len(peers))
        send_groups(n, sums)

        def local(q, carry):
            cols = pl.ds(pl.multiple_of(q * quarter, quarter), quarter)
            comp = comp_ref[:, cols]
            scaled = (dot(owner, comp) * rows[:, cols].astype(F32)).astype(BF16)
            loc[:, cols] = dot(gain_b, comp) * src[:, cols].astype(F32) - dot(mix[...], scaled)
            return carry

        lax.fori_loop(0, 4, local, 0)

    to = lax.broadcasted_iota(jnp.int32, (top_rows, 4 * devs * REST), 0)
    of = lax.broadcasted_iota(jnp.int32, (top_rows, 4 * devs * REST), 1)
    put_at = to % TOP // REST * (devs * REST) + to // TOP * REST + to % REST
    spread[...] = (of == put_at).astype(F32).astype(BF16)
    head(0, member_b, inverse, tok_ref, mix_out, loc_out)
    head(1, weight_b, None, cot_ref, mix_in, loc_in)
    relay_on(0)
    relay_on(1)
    sent(0, 0)
    for load in loads:
        load.wait()

    mine = counts_ref[2 * me]
    row_1 = lax.broadcasted_iota(jnp.int32, (all_rows, 1), 0)
    zero_exp = (row_1 < top_rows) & (row_1 % TOP < mine)
    step = 256
    arrive(0, 1)
    take_rows(0)

    def both(w, cols):
        return jnp.where(zero_exp, dot(rows[...], w[0, :, cols]), dot(rows[...], w[1, :, cols]))

    def split(ref, f, value):
        ref[:, pl.ds(f, step)] = jnp.where(zero_exp, value, 0.0).astype(BF16)
        ref[:, pl.ds(pl.multiple_of(f + ff, step), step)] = jnp.where(zero_exp, 0.0, value).astype(BF16)

    def forward(i, carry):
        f = pl.multiple_of(i * step, step)
        cols = pl.ds(f, step)
        g, u = both(wg, cols), both(wu, cols)
        gate[:, cols] = g.astype(BF16)
        up[:, cols] = u.astype(BF16)
        split(hid, f, g * jax.nn.sigmoid(g) * u)
        return carry

    lax.fori_loop(0, ff // step, forward, 0)

    def out_cols(g):
        w = jnp.concatenate([wd[:, cols] for cols in lanes(g)], axis=1)
        return dot(hid[...], w).astype(BF16)

    send_groups(2, out_cols)

    arrive(1, 1)
    sent(1, 0)
    take_rows(1)

    def y_copy(i):
        e, dest, sign, dst = (
            (0, 2, 1, relay.at[0]), (1, 2, NY - 1, relay.at[1]),
            (1, 1, 1, final.at[0, 1]), (0, NY - 1, NY - 1, final.at[1, 0]),
            (0, 1, 1, final.at[0, 0]), (1, NY - 1, NY - 1, final.at[1, 1]),
        )[i]
        return pltpu.make_async_remote_copy(
            src_ref=part.at[(y + dest) % NY, e], dst_ref=dst, send_sem=yss.at[i],
            recv_sem=yrs.at[i], device_id=y_dev(sign), device_id_type=MESH,
        )

    def down(shift):
        owner_y = (y + shift) % NY
        cols = pl.ds(pl.multiple_of(owner_y * quarter, quarter), quarter)

        def body(i, carry):
            f = pl.multiple_of(i * step, step)
            for e in range(2):
                at_f = pl.ds(pl.multiple_of(f + e * ff, step), step)
                part[owner_y, e, pl.ds(f, step), :] = dot(hid[:, at_f], rows[:, cols], 0, 0).astype(BF16)
            return carry

        lax.fori_loop(0, ff // step, body, 0)

    down(2)
    y_copy(0).start()
    y_copy(1).start()
    down(1)
    y_copy(2).start()
    down(NY - 1)
    y_copy(3).start()
    down(0)

    def backward(i, carry):
        f = pl.multiple_of(i * step, step)
        cols = pl.ds(f, step)
        high = pl.ds(pl.multiple_of(f + ff, step), step)
        dh = jnp.where(zero_exp, dot(rows[...], wd[cols, :], 1, 1), dot(rows[...], wd[high, :], 1, 1))
        g, u = gate[:, cols].astype(F32), up[:, cols].astype(F32)
        s = jax.nn.sigmoid(g)
        split(dgs, f, dh * u * s * (1.0 + g * (1.0 - s)))
        split(dus, f, dh * g * s)
        return carry

    lax.fori_loop(0, ff // step, backward, 0)
    relay_on(2)

    def back_cols(g):
        total = jnp.zeros((all_rows, quarter), F32)
        for e in range(2):
            half = slice(e * ff, (e + 1) * ff)
            for ref, w in ((dgs, wg), (dus, wu)):
                side = jnp.concatenate([w[e, cols, :] for cols in lanes(g)], axis=0)
                total += dot(ref[:, half], side, 1, 1)
        return total.astype(BF16)

    send_groups(3, back_cols)

    for i, shift, e in ((0, 1, 0), (1, NY - 1, 1)):
        y_copy(i).wait_recv()
        owner_y = (y + shift) % NY

        def add(j, carry):
            at_f = pl.ds(pl.multiple_of(j * step, step), step)
            total = part[owner_y, e, at_f, :].astype(F32) + relay[i, at_f, :].astype(F32)
            part[owner_y, e, at_f, :] = total.astype(BF16)
            return carry

        lax.fori_loop(0, ff // step, add, 0)
        y_copy(4 + i).start()
    relay_on(3)

    def tail(n, mix, loc, out_ref):
        arrive(n, 1)
        take_rows(n)

        def body(q, carry):
            cols = pl.ds(pl.multiple_of(q * quarter, quarter), quarter)
            out_ref[:, cols] = (loc[:, cols] + dot(mix[...], rows[:, cols])).astype(BF16)
            return carry

        lax.fori_loop(0, 4, body, 0)

    tail(2, mix_out, loc_out, layer_ref)
    for i in range(2, 6):
        y_copy(i).wait_recv()

    def finish(j, carry):
        at_f = pl.ds(pl.multiple_of(j * step, step), step)
        for e in range(2):
            total = part[y, e, at_f, :].astype(F32) + final[0, e, at_f, :].astype(F32)
            relay[e, at_f, :] = (total + final[1, e, at_f, :].astype(F32)).astype(BF16)
        return carry

    lax.fori_loop(0, ff // step, finish, 0)
    down_out = pltpu.make_async_copy(relay, down_hbm, osem)
    down_out.start()
    tail(3, mix_in, loc_in, grad_ref)
    for n in range(4):
        if n >= 2:
            sent(n, 0)
        sent(n, 1)
    for i in range(6):
        y_copy(i).wait_send()
    down_out.wait()


def ship(*refs):
    count = (len(refs) - 2) // 3
    srcs, dsts, bufs = (refs[i * count:(i + 1) * count] for i in range(3))
    in_sem, out_sem = refs[3 * count:]
    reads = [pltpu.make_async_copy(s, b, in_sem.at[i]) for i, (s, b) in enumerate(zip(srcs, bufs))]
    writes = [pltpu.make_async_copy(b, d, out_sem.at[i]) for i, (b, d) in enumerate(zip(bufs, dsts))]
    for read in reads:
        read.start()
    for read, write in zip(reads, writes):
        read.wait()
        write.start()
    for write in writes:
        write.wait()


def on_device(
    tokens, expert_ids, bucket_codes, route_weights, cotangent, counts, comp_scale, w_gate, w_up, w_down
):
    tok_n, width = tokens.shape
    local, _, ff = w_gate.shape
    devs = NZ * NX * NC
    all_rows, quarter = devs * PAIR, width // 4
    vmem = pl.BlockSpec(memory_space=pltpu.VMEM)
    hbm = pl.BlockSpec(memory_space=pl.ANY)
    mid = jax.ShapeDtypeStruct((4, NC, 4, NC, LINE, LANES), BF16)
    rows_buf = pltpu.VMEM((4, NZ, NX, NC, LINE, LANES), BF16)
    dma = pltpu.SemaphoreType.DMA
    out = pl.pallas_call(
        kernel,
        out_shape=[
            jax.ShapeDtypeStruct((tok_n, width), BF16),
            jax.ShapeDtypeStruct((tok_n, width), BF16),
            jax.ShapeDtypeStruct((local, ff, quarter), BF16),
        ] + [mid] * 8,
        in_specs=[pl.BlockSpec(memory_space=pltpu.SMEM)] + [vmem] * 6 + [hbm] * 3,
        out_specs=[vmem] * 2 + [hbm] * 9,
        scratch_shapes=[rows_buf] * 6 + [
            pltpu.VMEM((local, width, ff), BF16),
            pltpu.VMEM((local, width, ff), BF16),
            pltpu.VMEM((local * ff, width), BF16),
            pltpu.VMEM((all_rows, width), BF16),
            pltpu.VMEM((devs * TOP, 4 * devs * REST), BF16),
            pltpu.VMEM((all_rows, ff), BF16),
            pltpu.VMEM((all_rows, ff), BF16),
            pltpu.VMEM((all_rows, local * ff), BF16),
            pltpu.VMEM((all_rows, local * ff), BF16),
            pltpu.VMEM((all_rows, local * ff), BF16),
            pltpu.VMEM((NY, local, ff, quarter), BF16),
            pltpu.VMEM((2, ff, quarter), BF16),
            pltpu.VMEM((2, local, ff, quarter), BF16),
            pltpu.VMEM((tok_n, all_rows), BF16),
            pltpu.VMEM((tok_n, all_rows), BF16),
            pltpu.VMEM((tok_n, width), F32),
            pltpu.VMEM((tok_n, width), F32),
            dma((3,)), dma, dma((4, 2, 8)), dma((4, 2, 8)), dma((4, 2, 8)), dma((4, 2, 8)),
            dma((6,)), dma((6,)),
        ],
        compiler_params=pltpu.CompilerParams(
            collective_id=0, has_side_effects=True, vmem_limit_bytes=67043328
        ),
    )(
        counts, expert_ids.T, bucket_codes.T, route_weights.T, tokens, cotangent, comp_scale,
        w_gate, w_up, w_down.reshape(local * ff, width),
    )
    shapes = [jax.ShapeDtypeStruct(a.shape, a.dtype) for a in out[:3]]
    return tuple(pl.pallas_call(
        ship,
        out_shape=shapes,
        in_specs=[hbm] * 3,
        out_specs=[hbm] * 3,
        scratch_shapes=[pltpu.VMEM(a.shape, a.dtype) for a in shapes] + [dma((3,)), dma((3,))],
    )(*out[:3]))


def solution(mesh):
    rows = P(("dp", "expert"), None)
    stack = P("expert", None, None)
    return jax.shard_map(
        on_device,
        mesh=mesh,
        in_specs=(rows, rows, rows, rows, rows, P(), P(), stack, stack, stack),
        out_specs=(rows, rows, P("expert", None, "dp")),
        check_vma=False,
    )
```

```python
import functools

import jax
import jax.numpy as jnp
from jax import lax
from jax.experimental import pallas as pl
from jax.experimental.pallas import tpu as pltpu
from jax.sharding import PartitionSpec as P

MESH = pl.DeviceIdType.MESH
F32 = jnp.float32
BF16 = jnp.bfloat16
NZ, NX, NC, NY = 4, 4, 2, 4
PAIR = 20
TOP = 16
REST = PAIR - TOP
LINE = 4 * PAIR
LANES = 128
FAR = (2, 1, 3, 0)


def dot(a, b, ca=1, cb=0):
    return lax.dot_general(a, b, (((ca,), (cb,)), ((), ())), preferred_element_type=F32)


def kernel(
    counts_ref, ids_ref, codes_ref, route_ref, tok_ref, cot_ref, comp_ref, wg_hbm, wu_hbm, wd_hbm,
    layer_ref, grad_ref, down_hbm, mid_a0, mid_a1, mid_b0, mid_b1, mid_c0, mid_c1, mid_d0, mid_d1,
    send_0, send_1, got_a, got_b, got_c, got_d, wg, wu, wd, rows, spread, gate, up, hid, dgs, dus,
    part, relay, final, mix_out, mix_in, loc_out, loc_in, wsem, osem, ss1, rs1, ss2, rs2, yss, yrs,
):
    devs = NZ * NX * NC
    top_rows, all_rows = devs * TOP, devs * PAIR
    tok_n, width = tok_ref.shape
    quarter = width // 4
    ff = wg.shape[2]
    me, y = lax.axis_index("expert"), lax.axis_index("dp")
    c, x, z = me % NC, (me // NC) % NX, me // (NC * NX)

    def at(zz, xx, cc):
        return {"expert": (zz * NX + xx) * NC + cc}

    def x_dev(dx, dc, back=False):
        return at(z, (x + (NX - dx if back else dx)) % NX, (c + dc) % NC)

    def z_dev(dz, dc, back=False):
        return at((z + (NZ - dz if back else dz)) % NZ, x, (c + dc) % NC)

    def y_dev(dy):
        return {"dp": (y + dy) % NY}

    peers = [x_dev(d, k) for d in range(NX) for k in range(NC) if d + k]
    peers += [z_dev(d, k) for d in range(1, NZ) for k in range(NC)]
    peers += [y_dev(1), y_dev(NY - 1)]
    barrier = pltpu.get_barrier_semaphore()
    for peer in peers:
        pl.semaphore_signal(barrier, inc=1, device_id=peer, device_id_type=MESH)

    loads = [
        pltpu.make_async_copy(src, dst, wsem.at[i])
        for i, (src, dst) in enumerate(((wg_hbm, wg), (wu_hbm, wu), (wd_hbm, wd)))
    ]
    for load in loads:
        load.start()

    sends = (send_0, send_1, send_0, send_1)
    mids = ((mid_a0, mid_a1), (mid_b0, mid_b1), (mid_c0, mid_c1), (mid_d0, mid_d1))
    gots = (got_a, got_b, got_c, got_d)

    def move(n, phase, side, d, k, here):
        buf, (mid_x, mid_z), got = sends[n], mids[n], gots[n]
        ssem, rsem = ((ss1, rs1), (ss2, rs2))[phase]
        cc, xx, zz = (c + k) % NC, (x + d) % NX, (z + d) % NZ
        if phase == 0 and side == 0:
            src, dst = buf.at[cc, :, xx], mid_x.at[x, c]
        elif phase == 0:
            src, dst = buf.at[NC + cc, zz], mid_z.at[z, c]
        elif side == 0:
            src, dst = mid_z.at[:, :, xx, cc], got.at[NC + c, :, x]
        else:
            src, dst = mid_x.at[:, :, zz, cc], got.at[c, z]
        i = d * NC + k
        if here:
            return pltpu.make_async_copy(src, dst, rsem.at[n, side, i])
        return pltpu.make_async_remote_copy(
            src_ref=src, dst_ref=dst, send_sem=ssem.at[n, side, i], recv_sem=rsem.at[n, side, i],
            device_id=(z_dev if side else x_dev)(d, k), device_id_type=MESH,
        )

    def copies(n, phase):
        return [
            [functools.partial(move, n, phase, side, d, k, d + k == 0) for d in FAR for k in (1, 0)]
            for side in range(2)
        ]

    def start(n, phase, sides=(0, 1)):
        both = copies(n, phase)
        for i in range(len(both[0])):
            for side in sides:
                both[side][i]().start()

    def arrive(n, phase, sides=(0, 1)):
        both = copies(n, phase)
        for side in sides:
            for copy in both[side][:-1]:
                copy().wait_recv()
            both[side][-1]().wait()

    def sent(n, phase):
        for side in copies(n, phase):
            for copy in side[:-1]:
                copy().wait_send()

    def relay_on(n):
        arrive(n, 0, (0,))
        start(n, 1, (1,))
        arrive(n, 0, (1,))
        start(n, 1, (0,))

    def pick(q, rows_n, cols_n, flip):
        i = lax.broadcasted_iota(jnp.int32, (rows_n, cols_n), 1 if flip else 0)
        j = lax.broadcasted_iota(jnp.int32, (rows_n, cols_n), 0 if flip else 1)
        return (j == (i // REST) * TOP + q * REST + i % REST).astype(F32).astype(BF16)

    def lanes(g):
        return [pl.ds(pl.multiple_of(q * quarter + g * LANES, LANES), LANES) for q in range(4)]

    def send_groups(n, value_of):
        buf = sends[n]

        def body(j, carry):
            cc = (c + 1 - j) % NC
            for side in range(2):
                g = side * NC + cc
                value = value_of(g)
                cuts = [slice(q * LANES, (q + 1) * LANES) for q in range(4)]
                for q in range(4):
                    top = value[:top_rows, cuts[q]]
                    buf[g, :, :, :, q * TOP:(q + 1) * TOP, :] = top.reshape(NZ, NX, NC, TOP, LANES)
                rest = jnp.concatenate([value[top_rows:, cuts[q]] for q in range(4)], axis=0)
                rest = dot(spread[...], rest).astype(BF16)
                buf[g, :, :, :, 4 * TOP:, :] = rest.reshape(NZ, NX, NC, TOP, LANES)
                for d in FAR[:3]:
                    move(n, 0, side, d, 1 - j, False).start()

                @pl.when(j == 0)
                def _():
                    move(n, 0, side, 0, 1, False).start()

                @pl.when(j == 1)
                def _():
                    move(n, 0, side, 0, 0, True).start()
            return carry

        lax.fori_loop(0, NC, body, 0)

    def take_rows(n):
        got = gots[n]

        def body(q, carry):
            at_q = pl.ds(pl.multiple_of(q * TOP, TOP), TOP)
            col = pl.multiple_of(q * quarter, quarter)
            sel = pick(q, devs * REST, top_rows, False)
            for g in range(4):
                lanes = pl.ds(pl.multiple_of(col + g * LANES, LANES), LANES)
                rows[:top_rows, lanes] = got[g, :, :, :, at_q, :].reshape(top_rows, LANES)
            rest = jnp.concatenate(
                [got[g, :, :, :, 4 * TOP:, :].reshape(top_rows, LANES) for g in range(4)], axis=1
            )
            rows[top_rows:, pl.ds(col, quarter)] = dot(sel, rest).astype(BF16)
            return carry

        lax.fori_loop(0, 4, body, 0)

    ids, codes, route = ids_ref[...], codes_ref[...], route_ref[...]
    experts = 2 * devs
    size = jnp.ones_like(ids)
    base = jnp.zeros_like(ids)
    for e in range(experts):
        hit = ids == e
        size = jnp.where(hit, counts_ref[e], size)
        if e % 2:
            base = jnp.where(hit, counts_ref[e - 1], base)
    code_f, size_f = codes.astype(F32), size.astype(F32)
    bucket = base + codes - jnp.floor((code_f + 0.5) / size_f).astype(jnp.int32) * size
    dest = ids // 2
    row_id = jnp.where(bucket < TOP, dest * TOP + bucket, top_rows + dest * REST + bucket - TOP)
    row_iota = lax.broadcasted_iota(jnp.int32, (all_rows, tok_n), 0)
    member = jnp.zeros((all_rows, tok_n), F32)
    weight = jnp.zeros((all_rows, tok_n), F32)
    e_iota = lax.broadcasted_iota(jnp.int32, (experts, tok_n), 0)
    gain = jnp.zeros((experts, tok_n), F32)
    for k in range(ids.shape[0]):
        hit = row_iota == row_id[k:k + 1, :]
        member = jnp.where(hit, 1.0, member)
        weight = jnp.where(hit, route[k:k + 1, :], weight)
        gain = jnp.where(e_iota == ids[k:k + 1, :], route[k:k + 1, :], gain)
    inverse = 1.0 / jnp.maximum(jnp.sum(member, axis=1, keepdims=True), 1.0)
    member_b, weight_b = member.astype(BF16), weight.astype(BF16)
    mix_out[...] = weight.T.astype(BF16)
    mix_in[...] = (member * inverse).T.astype(BF16)
    gain_b = gain.T.astype(BF16)

    row_e = lax.broadcasted_iota(jnp.int32, (all_rows, experts), 0)
    col_e = lax.broadcasted_iota(jnp.int32, (all_rows, experts), 1)
    row_dest = jnp.where(row_e < top_rows, row_e // TOP, (row_e - top_rows) // REST)
    row_bucket = jnp.where(row_e < top_rows, row_e % TOP, TOP)
    first = lax.broadcasted_iota(jnp.int32, (1, experts), 1)
    first_n = jnp.zeros((1, experts), jnp.int32)
    for j in range(devs):
        first_n = jnp.where(first // 2 == j, counts_ref[2 * j], first_n)
    owner = jnp.where(
        (col_e // 2 == row_dest) & ((row_bucket >= first_n) == (col_e % 2 == 1)), 1.0, 0.0
    ).astype(BF16)

    def head(n, lhs, scale, src, mix, loc):
        def sums(g):
            value = dot(lhs, jnp.concatenate([src[:, cols] for cols in lanes(g)], axis=1))
            if scale is not None:
                value = value * scale
            value = value.astype(BF16)
            for q, cols in enumerate(lanes(g)):
                rows[:, cols] = value[:, q * LANES:(q + 1) * LANES]
            return value

        if n == 0:
            pl.semaphore_wait(barrier, len(peers))
        send_groups(n, sums)

        def local(q, carry):
            cols = pl.ds(pl.multiple_of(q * quarter, quarter), quarter)
            comp = comp_ref[:, cols]
            scaled = (dot(owner, comp) * rows[:, cols].astype(F32)).astype(BF16)
            loc[:, cols] = dot(gain_b, comp) * src[:, cols].astype(F32) - dot(mix[...], scaled)
            return carry

        lax.fori_loop(0, 4, local, 0)

    to = lax.broadcasted_iota(jnp.int32, (top_rows, 4 * devs * REST), 0)
    of = lax.broadcasted_iota(jnp.int32, (top_rows, 4 * devs * REST), 1)
    put_at = to % TOP // REST * (devs * REST) + to // TOP * REST + to % REST
    spread[...] = (of == put_at).astype(F32).astype(BF16)
    head(0, member_b, inverse, tok_ref, mix_out, loc_out)
    head(1, weight_b, None, cot_ref, mix_in, loc_in)
    relay_on(0)
    relay_on(1)
    sent(0, 0)
    for load in loads:
        load.wait()

    mine = counts_ref[2 * me]
    row_1 = lax.broadcasted_iota(jnp.int32, (all_rows, 1), 0)
    zero_exp = (row_1 < top_rows) & (row_1 % TOP < mine)
    step = 256
    arrive(0, 1)
    take_rows(0)

    def both(w, cols):
        return jnp.where(zero_exp, dot(rows[...], w[0, :, cols]), dot(rows[...], w[1, :, cols]))

    def split(ref, f, value):
        ref[:, pl.ds(f, step)] = jnp.where(zero_exp, value, 0.0).astype(BF16)
        ref[:, pl.ds(pl.multiple_of(f + ff, step), step)] = jnp.where(zero_exp, 0.0, value).astype(BF16)

    def forward(i, carry):
        f = pl.multiple_of(i * step, step)
        cols = pl.ds(f, step)
        g, u = both(wg, cols), both(wu, cols)
        gate[:, cols] = g.astype(BF16)
        up[:, cols] = u.astype(BF16)
        split(hid, f, g * jax.nn.sigmoid(g) * u)
        return carry

    lax.fori_loop(0, ff // step, forward, 0)

    def out_cols(g):
        w = jnp.concatenate([wd[:, cols] for cols in lanes(g)], axis=1)
        return dot(hid[...], w).astype(BF16)

    send_groups(2, out_cols)

    arrive(1, 1)
    sent(1, 0)
    take_rows(1)

    def y_copy(i):
        e, dest, sign, dst = (
            (0, 2, 1, relay.at[0]), (1, 2, NY - 1, relay.at[1]),
            (1, 1, 1, final.at[0, 1]), (0, NY - 1, NY - 1, final.at[1, 0]),
            (0, 1, 1, final.at[0, 0]), (1, NY - 1, NY - 1, final.at[1, 1]),
        )[i]
        return pltpu.make_async_remote_copy(
            src_ref=part.at[(y + dest) % NY, e], dst_ref=dst, send_sem=yss.at[i],
            recv_sem=yrs.at[i], device_id=y_dev(sign), device_id_type=MESH,
        )

    def down(shift):
        owner_y = (y + shift) % NY
        cols = pl.ds(pl.multiple_of(owner_y * quarter, quarter), quarter)

        def body(i, carry):
            f = pl.multiple_of(i * step, step)
            for e in range(2):
                at_f = pl.ds(pl.multiple_of(f + e * ff, step), step)
                part[owner_y, e, pl.ds(f, step), :] = dot(hid[:, at_f], rows[:, cols], 0, 0).astype(BF16)
            return carry

        lax.fori_loop(0, ff // step, body, 0)

    down(2)
    y_copy(0).start()
    y_copy(1).start()
    down(1)
    y_copy(2).start()
    down(NY - 1)
    y_copy(3).start()

    def backward(i, carry):
        f = pl.multiple_of(i * step, step)
        cols = pl.ds(f, step)
        high = pl.ds(pl.multiple_of(f + ff, step), step)
        dh = jnp.where(zero_exp, dot(rows[...], wd[cols, :], 1, 1), dot(rows[...], wd[high, :], 1, 1))
        g, u = gate[:, cols].astype(F32), up[:, cols].astype(F32)
        s = jax.nn.sigmoid(g)
        split(dgs, f, dh * u * s * (1.0 + g * (1.0 - s)))
        split(dus, f, dh * g * s)
        return carry

    lax.fori_loop(0, ff // step, backward, 0)
    relay_on(2)

    def back_cols(g):
        total = jnp.zeros((all_rows, quarter), F32)
        for e in range(2):
            half = slice(e * ff, (e + 1) * ff)
            for ref, w in ((dgs, wg), (dus, wu)):
                side = jnp.concatenate([w[e, cols, :] for cols in lanes(g)], axis=0)
                total += dot(ref[:, half], side, 1, 1)
        return total.astype(BF16)

    send_groups(3, back_cols)
    down(0)

    for i, shift, e in ((0, 1, 0), (1, NY - 1, 1)):
        y_copy(i).wait_recv()
        owner_y = (y + shift) % NY

        def add(j, carry):
            at_f = pl.ds(pl.multiple_of(j * step, step), step)
            total = part[owner_y, e, at_f, :].astype(F32) + relay[i, at_f, :].astype(F32)
            part[owner_y, e, at_f, :] = total.astype(BF16)
            return carry

        lax.fori_loop(0, ff // step, add, 0)
        y_copy(4 + i).start()
    relay_on(3)

    def tail(n, mix, loc, out_ref):
        arrive(n, 1)
        take_rows(n)

        def body(q, carry):
            cols = pl.ds(pl.multiple_of(q * quarter, quarter), quarter)
            out_ref[:, cols] = (loc[:, cols] + dot(mix[...], rows[:, cols])).astype(BF16)
            return carry

        lax.fori_loop(0, 4, body, 0)

    tail(2, mix_out, loc_out, layer_ref)
    for i in range(2, 6):
        y_copy(i).wait_recv()

    def finish(j, carry):
        at_f = pl.ds(pl.multiple_of(j * step, step), step)
        for e in range(2):
            total = part[y, e, at_f, :].astype(F32) + final[0, e, at_f, :].astype(F32)
            relay[e, at_f, :] = (total + final[1, e, at_f, :].astype(F32)).astype(BF16)
        return carry

    lax.fori_loop(0, ff // step, finish, 0)
    down_out = pltpu.make_async_copy(relay, down_hbm, osem)
    down_out.start()
    tail(3, mix_in, loc_in, grad_ref)
    for n in range(4):
        if n >= 2:
            sent(n, 0)
        sent(n, 1)
    for i in range(6):
        y_copy(i).wait_send()
    down_out.wait()


def ship(*refs):
    count = (len(refs) - 2) // 3
    srcs, dsts, bufs = (refs[i * count:(i + 1) * count] for i in range(3))
    in_sem, out_sem = refs[3 * count:]
    reads = [pltpu.make_async_copy(s, b, in_sem.at[i]) for i, (s, b) in enumerate(zip(srcs, bufs))]
    writes = [pltpu.make_async_copy(b, d, out_sem.at[i]) for i, (b, d) in enumerate(zip(bufs, dsts))]
    for read in reads:
        read.start()
    for read, write in zip(reads, writes):
        read.wait()
        write.start()
    for write in writes:
        write.wait()


def on_device(
    tokens, expert_ids, bucket_codes, route_weights, cotangent, counts, comp_scale, w_gate, w_up, w_down
):
    tok_n, width = tokens.shape
    local, _, ff = w_gate.shape
    devs = NZ * NX * NC
    all_rows, quarter = devs * PAIR, width // 4
    vmem = pl.BlockSpec(memory_space=pltpu.VMEM)
    hbm = pl.BlockSpec(memory_space=pl.ANY)
    mid = jax.ShapeDtypeStruct((4, NC, 4, NC, LINE, LANES), BF16)
    rows_buf = pltpu.VMEM((4, NZ, NX, NC, LINE, LANES), BF16)
    dma = pltpu.SemaphoreType.DMA
    out = pl.pallas_call(
        kernel,
        out_shape=[
            jax.ShapeDtypeStruct((tok_n, width), BF16),
            jax.ShapeDtypeStruct((tok_n, width), BF16),
            jax.ShapeDtypeStruct((local, ff, quarter), BF16),
        ] + [mid] * 8,
        in_specs=[pl.BlockSpec(memory_space=pltpu.SMEM)] + [vmem] * 6 + [hbm] * 3,
        out_specs=[vmem] * 2 + [hbm] * 9,
        scratch_shapes=[rows_buf] * 6 + [
            pltpu.VMEM((local, width, ff), BF16),
            pltpu.VMEM((local, width, ff), BF16),
            pltpu.VMEM((local * ff, width), BF16),
            pltpu.VMEM((all_rows, width), BF16),
            pltpu.VMEM((devs * TOP, 4 * devs * REST), BF16),
            pltpu.VMEM((all_rows, ff), BF16),
            pltpu.VMEM((all_rows, ff), BF16),
            pltpu.VMEM((all_rows, local * ff), BF16),
            pltpu.VMEM((all_rows, local * ff), BF16),
            pltpu.VMEM((all_rows, local * ff), BF16),
            pltpu.VMEM((NY, local, ff, quarter), BF16),
            pltpu.VMEM((2, ff, quarter), BF16),
            pltpu.VMEM((2, local, ff, quarter), BF16),
            pltpu.VMEM((tok_n, all_rows), BF16),
            pltpu.VMEM((tok_n, all_rows), BF16),
            pltpu.VMEM((tok_n, width), F32),
            pltpu.VMEM((tok_n, width), F32),
            dma((3,)), dma, dma((4, 2, 8)), dma((4, 2, 8)), dma((4, 2, 8)), dma((4, 2, 8)),
            dma((6,)), dma((6,)),
        ],
        compiler_params=pltpu.CompilerParams(
            collective_id=0, has_side_effects=True, vmem_limit_bytes=67043328
        ),
    )(
        counts, expert_ids.T, bucket_codes.T, route_weights.T, tokens, cotangent, comp_scale,
        w_gate, w_up, w_down.reshape(local * ff, width),
    )
    shapes = [jax.ShapeDtypeStruct(a.shape, a.dtype) for a in out[:3]]
    return tuple(pl.pallas_call(
        ship,
        out_shape=shapes,
        in_specs=[hbm] * 3,
        out_specs=[hbm] * 3,
        scratch_shapes=[pltpu.VMEM(a.shape, a.dtype) for a in shapes] + [dma((3,)), dma((3,))],
    )(*out[:3]))


def solution(mesh):
    rows = P(("dp", "expert"), None)
    stack = P("expert", None, None)
    return jax.shard_map(
        on_device,
        mesh=mesh,
        in_specs=(rows, rows, rows, rows, rows, P(), P(), stack, stack, stack),
        out_specs=(rows, rows, P("expert", None, "dp")),
        check_vma=False,
    )
```
